32 devices in a mesh: row: 8 (over y, x, core), col: 4 (over z).
Axes of the slice: x: 2, y: 2, z: 4, core: 2. Of those that a mesh axis runs over, the one named last changes fastest.
Arguments:
- question_vectors: bfloat16 [512, 2048], P('row', 'col'), may hold values from -0.5 to 0.5
- document_vectors: bfloat16 [512, 2048], P('col', 'row'), may hold values from -0.5 to 0.5
- positive: int32 [512], P('row'), may hold values from 0 to 511
- tokens: bfloat16 [4096, 2048], P(('row', 'col')), may hold values from -6 to 6
- expert_ids: int32 [4096, 8], P(('row', 'col')), may hold values from 0 to 31, all different within a row; in each aligned block of 128 rows (0 to 127, 128 to 255, ...) at most 36 rows name the same one
- route_weights: float32 [4096, 8], P(('row', 'col')), may hold values from 0.03 to 0.3
- expert_gate_up: bfloat16 [32, 2048, 1536], P(('row', 'col')), may hold values from -0.125 to 0.125
- expert_down: bfloat16 [32, 768, 2048], P(('row', 'col')), may hold values from -0.21875 to 0.21875
Outputs:
- passage_grad: float32 [512, 2048], P('col', 'row')
- token_grad: bfloat16 [4096, 2048], P(('row', 'col'))
- gate_up_grad: bfloat16 [32, 2048, 1536], P(('row', 'col'))
- down_grad: bfloat16 [32, 768, 2048], P(('row', 'col'))
The draws below stay inside these ranges and needn't reach their ends.
Inputs may be any that keep to these rules, and one draw needn't show every extreme that they name: `expert_ids`: each token names 8 different experts; among the 128 tokens of one device no expert is named more than 36 times, a bound that some block reaches.
All inputs are finite; a program needn't handle non-finite values.
Results may differ from the reference program's by a relative error of at most 0.018.
Values may be sent and summed in bfloat16 or wider, within the bound.
A program may use at most 192 MiB of HBM per device.

```python
import math
import jax
import jax.numpy as jnp
import numpy as np
from jax import lax

D = 2048
FF = 768
TOP = 8
SEQ_LEN = 8
TOK_DEV = 128
TOKENS = 4096
NQ = 512
NP = 512
EXPERTS = 32
CAP = 36
DEVICES = 32


sharpness_divisor = 0.02


def embed_pair(key):
    folded = jax.random.fold_in(key, 4099)
    subkeys = jax.random.split(folded, 9)
    question_vectors = jax.random.normal(subkeys[0], (NQ, D), jnp.float32) * 0.03
    document_vectors = jax.random.normal(subkeys[1], (NP, D), jnp.float32) * 0.03
    chosen_q = jax.random.permutation(subkeys[4], NQ)[:8]
    chosen_p = jax.random.permutation(subkeys[5], NP)[:16]
    sign_pattern = jax.random.randint(subkeys[6], (8, D), 0, 2).astype(jnp.float32) * 2.0 - 1.0
    direction_unit = sign_pattern / math.sqrt(D)
    correct_classes = jnp.array([110.0, 170.0, 230.0, 290.0, 140.0, 200.0, 260.0, 320.0], jnp.float32)
    magnitude = jnp.sqrt(correct_classes * sharpness_divisor)[:, None]
    query_planted = magnitude * direction_unit
    passage_planted = magnitude * direction_unit
    interval_lengths = jax.random.uniform(subkeys[7], (8,), jnp.float32, 1.0, 3.0)
    query_power = jnp.sum(query_planted * query_planted, axis=1, keepdims=True)
    jitter_shift = jax.random.normal(subkeys[8], (8, D), jnp.float32) * (0.2 / math.sqrt(D))
    jitter_shift = jitter_shift - jnp.sum(jitter_shift * query_planted, axis=1, keepdims=True) / query_power * query_planted
    distractor_vector = passage_planted - interval_lengths[:, None] * sharpness_divisor * query_planted / query_power + jitter_shift
    question_vectors = question_vectors.at[chosen_q].set(query_planted)
    document_vectors = document_vectors.at[chosen_p[:8]].set(passage_planted)
    document_vectors = document_vectors.at[chosen_p[8:]].set(distractor_vector)
    return (jnp.clip(question_vectors, -0.5, 0.5), jnp.clip(document_vectors, -0.5, 0.5))


def draw_question_vectors(key, part):
    return embed_pair(key)[0].astype(jnp.bfloat16)


def draw_document_vectors(key, part):
    return embed_pair(key)[1].astype(jnp.bfloat16)


def touch_ends(entries, stream_key, least, top_value):
    longest = entries.shape.index(max(entries.shape))
    spots = []
    for shift in (0, 1):
        where = [jax.random.randint(jax.random.fold_in(stream_key, axis), (), 0, length) for axis, length in enumerate(entries.shape)]
        where[longest] = (where[longest] + shift) % entries.shape[longest]
        spots.append(tuple(where))
    return entries.at[spots[0]].set(least).at[spots[1]].set(top_value)


def block_levels(key, shape, cuts, smallest, largest):
    loudness = 1.0
    for dim, blocks in cuts:
        steps = jax.random.uniform(jax.random.fold_in(jax.random.fold_in(key, 6), dim), (blocks,), jnp.float32, smallest / len(cuts), largest / len(cuts))
        loudness = loudness * jnp.repeat(jnp.exp(steps), shape[dim] // blocks).reshape((-1,) + (1,) * (len(shape) - 1 - dim))
    return loudness


def routed_block(rng, own, number, rows, amount, top, limit, skew):
    order = jax.random.permutation(rng, amount)
    crowded, usual = shares(amount, rows * top, limit, skew, True), shares(amount, rows * top, limit, skew, False)
    places = jnp.arange(amount)

    def named(tallies, offset_by):
        used = int((tallies > 0).sum())
        fixed = max(1, used // 4)
        shifted = fixed + (places - fixed + offset_by * (used - fixed)) % max(1, amount - fixed)
        return jnp.zeros((amount,), jnp.int32).at[order[jnp.where(places < fixed, places, shifted)]].set(jnp.asarray(tallies, jnp.int32))

    tallies = jnp.where(number % 4 == 0, named(crowded, number // 4), named(usual, number - number // 4 - 1))
    mixed = jax.random.permutation(jax.random.fold_in(own, 3), amount)
    donor, receiver = mixed[0:amount // 2 * 2:2], mixed[1:amount // 2 * 2:2]
    margin = jnp.minimum(tallies[donor] - 1, limit - tallies[receiver]) // 2
    margin = jnp.where((donor == order[0]) | (receiver == order[0]) | (tallies[receiver] == 0), 0, jnp.maximum(margin, 0))
    shifted = jax.random.randint(jax.random.fold_in(own, 4), (amount // 2,), 0, 1 << 20) % (margin + 1)
    tallies = tallies.at[donor].add(-shifted).at[receiver].add(shifted)
    members = jnp.searchsorted(jnp.cumsum(tallies), jnp.arange(rows * top), side="right").astype(jnp.int32)
    table = members.reshape(top, rows).T
    table = table[jax.random.permutation(jax.random.fold_in(own, 1), rows)]
    offset_by = jax.random.randint(jax.random.fold_in(own, 2), (rows, 1), 0, top)
    return jnp.take_along_axis(table, (jnp.arange(top)[None, :] + offset_by) % top, axis=1)


def shares(amount, total, limit, skew, full):
    weights = [(1 << 20) // math.isqrt(grade ** skew) + 1 for grade in range(1, amount + 1)]
    largest = limit if full else min(limit, max(-(-total // amount), total * weights[0] // sum(weights)))
    least = 1 if total - largest >= amount - 1 else 0
    counts, spare = [largest] + [least] * (amount - 1), total - largest - least * (amount - 1)
    while spare > 0:
        candidates = [i for i in range(1, amount) if counts[i] < largest] or [i for i in range(1, amount) if counts[i] < limit]
        whole, budget = sum([weights[i] for i in candidates]), spare
        for i in candidates:
            extra = min(limit - counts[i], max(1, budget * weights[i] // whole), spare)
            counts[i] = counts[i] + extra
            spare = spare - extra
    return np.array(counts)


def gaussian(own_key, extent, scale, most, pieces=(), held_as=jnp.bfloat16):
    values = scale * jax.random.normal(own_key, extent, jnp.float32)
    if pieces:
        values = values * block_levels(own_key, extent, pieces, -0.22, 0.18)
    return jnp.clip(values, -most, most).astype(held_as)


def setup_inputs(seed: int = 0) -> dict:
    key_list = jax.random.split(jax.random.key(seed), 9)
    question_vectors = draw_question_vectors(jax.random.fold_in(key_list[8], 71), 0)
    document_vectors = draw_document_vectors(jax.random.fold_in(key_list[8], 71), 0)
    positive = touch_ends(jax.random.randint(key_list[2], (NQ,), 0, NP), jax.random.fold_in(key_list[2], 1), 0, NP - 1).astype(jnp.int32)
    tokens = gaussian(key_list[3], (TOKENS, D), 1.0, 6.0, ((0, 32),))
    expert_ids_keys = jax.random.split(jax.random.fold_in(key_list[4], 1), TOKENS // TOK_DEV)
    expert_ids_turns = jax.random.permutation(jax.random.fold_in(key_list[4], 3), TOKENS // TOK_DEV)
    expert_ids = jax.vmap(lambda own, number: routed_block(jax.random.fold_in(key_list[4], 2), own, number, TOK_DEV, EXPERTS, TOP, CAP, 1))(expert_ids_keys, expert_ids_turns).reshape((TOKENS, TOP))
    route_weights = jnp.clip(jnp.exp(math.log(0.3) - 2.3025852 * jax.random.uniform(key_list[5], (TOKENS, TOP), jnp.float32) ** block_levels(key_list[5], (TOKENS, TOP), ((0, 32),), -0.2, 0.2)), 0.03, 0.3)
    expert_gate_up = gaussian(key_list[6], (EXPERTS, D, 2 * FF), D ** -0.5, 0.125, ((0, 32),))
    expert_down = gaussian(key_list[7], (EXPERTS, FF, D), FF ** -0.5, 0.21875, ((0, 32),))
    return dict(question_vectors=question_vectors, document_vectors=document_vectors, positive=positive, tokens=tokens, expert_ids=expert_ids, route_weights=route_weights, expert_gate_up=expert_gate_up, expert_down=expert_down)


sharpness_divisor = 0.02


def expert_backward(slot_inputs, slot_grads, gate_up, down_proj):
    projected = jnp.dot(slot_inputs, gate_up, preferred_element_type=jnp.float32)
    hidden_width = down_proj.shape[0]
    gate_part = projected[:, :hidden_width]
    up_part = projected[:, hidden_width:]
    sigmoid_gate = jax.nn.sigmoid(gate_part)
    activated = gate_part * sigmoid_gate
    hidden = (activated * up_part).astype(jnp.bfloat16)
    down_grad = lax.dot_general(hidden, slot_grads, (((0,), (0,)), ((), ())), preferred_element_type=jnp.float32).astype(jnp.bfloat16)
    hidden_grad = lax.dot_general(slot_grads, down_proj, (((1,), (1,)), ((), ())), preferred_element_type=jnp.float32)
    slope = sigmoid_gate * (1.0 + gate_part * (1.0 - sigmoid_gate))
    pre_grad = jnp.concatenate([hidden_grad * up_part * slope, hidden_grad * activated], axis=1).astype(jnp.bfloat16)
    gate_up_grad = lax.dot_general(slot_inputs, pre_grad, (((0,), (0,)), ((), ())), preferred_element_type=jnp.float32).astype(jnp.bfloat16)
    input_grad = lax.dot_general(pre_grad, gate_up, (((1,), (1,)), ((), ())), preferred_element_type=jnp.float32).astype(jnp.bfloat16)
    return input_grad, gate_up_grad, down_grad


def reference(question_vectors, document_vectors, positive, tokens, expert_ids, route_weights, expert_gate_up, expert_down):
    similarity_entries = jnp.dot(question_vectors, document_vectors.T, preferred_element_type=jnp.float32) / sharpness_divisor
    row_peak = jnp.max(similarity_entries, axis=1, keepdims=True)
    coefficient_entries = jnp.exp(similarity_entries - row_peak)
    partition_normalizer = jnp.sum(coefficient_entries, axis=1, keepdims=True)
    columns = jnp.arange(NP, dtype=jnp.int32)
    membership_table = (positive[:, None] == columns[None, :]).astype(jnp.float32)
    similarity_derivative = ((coefficient_entries / partition_normalizer - membership_table) / sharpness_divisor).astype(jnp.bfloat16)
    query_grad = jnp.dot(similarity_derivative, document_vectors, preferred_element_type=jnp.float32)
    passage_grad = jnp.dot(similarity_derivative.T, question_vectors, preferred_element_type=jnp.float32)
    cotangent = jnp.repeat(query_grad / SEQ_LEN, SEQ_LEN, axis=0).astype(jnp.bfloat16)

    blocks = expert_ids.reshape(DEVICES, TOK_DEV * TOP)
    expert_hit = (blocks[:, :, None] == jnp.arange(EXPERTS, dtype=jnp.int32)[None, None, :]).astype(jnp.int32)
    before = jnp.cumsum(expert_hit, axis=1) - expert_hit
    slot_number = jnp.sum(before * expert_hit, axis=2)
    source = jnp.arange(DEVICES, dtype=jnp.int32)[:, None]
    slot_index = (blocks * (DEVICES * CAP) + source * CAP + slot_number).reshape(-1).astype(jnp.int32)
    slot_owner = jnp.full((EXPERTS * DEVICES * CAP,), -1, jnp.int32)
    slot_owner = slot_owner.at[slot_index].set(jnp.arange(TOKENS * TOP, dtype=jnp.int32))
    slot_owner = slot_owner.reshape(EXPERTS, DEVICES * CAP)
    flat_weights = route_weights.reshape(-1)

    def per_expert(carried, inputs):
        owners, gate_up, down_proj = inputs
        filled = owners >= 0
        pair_row = jnp.maximum(owners, 0).astype(jnp.int32)
        token_row = (pair_row // TOP).astype(jnp.int32)
        slot_inputs = jnp.where(filled[:, None], tokens[token_row], jnp.zeros((), tokens.dtype))
        scaled = jnp.where(filled, flat_weights[pair_row], jnp.zeros((), flat_weights.dtype))
        slot_grads = (scaled[:, None] * cotangent[token_row].astype(jnp.float32)).astype(jnp.bfloat16)
        input_grad, gate_up_grad, down_grad = expert_backward(slot_inputs, slot_grads, gate_up, down_proj)
        addend = jnp.where(filled[:, None], input_grad.astype(jnp.float32), jnp.zeros((), jnp.float32))
        carried = carried.at[token_row].add(addend)
        return carried, (gate_up_grad, down_grad)

    start_grad = jnp.zeros((TOKENS, D), jnp.float32)
    summed, (gate_up_grad, down_grad) = lax.scan(per_expert, start_grad, (slot_owner, expert_gate_up, expert_down))
    token_grad = (cotangent.astype(jnp.float32) + summed).astype(jnp.bfloat16)
    return passage_grad, token_grad, gate_up_grad, down_grad
```

```python
import jax
import jax.numpy as jnp
from jax import lax
from jax.sharding import PartitionSpec as P

SEQ_LEN = 8


sharpness_divisor = 0.02

BF = jnp.bfloat16
F32 = jnp.float32


def contract(a, b, da, db):
    return lax.dot_general(a, b, (((da,), (db,)), ((), ())), preferred_element_type=F32)


def slot_counts(hit):
    tok = hit.shape[1]
    earlier = (
        lax.broadcasted_iota(jnp.int32, (tok, tok), 0)
        < lax.broadcasted_iota(jnp.int32, (tok, tok), 1)
    ).astype(BF)
    return contract(hit.astype(BF), earlier, 1, 0).astype(jnp.int32)


def shards(
    question_vectors,
    document_vectors,
    positive,
    tokens,
    expert_ids,
    route_weights,
    expert_gate_up,
    expert_down,
):
    row_size = lax.axis_size("row")
    col_size = lax.axis_size("col")
    row = lax.axis_index("row")
    col = lax.axis_index("col")
    devices_all = row_size * col_size
    me = row * col_size + col
    tok_count, model_width = tokens.shape
    top_count = expert_ids.shape[1]
    experts_all = devices_all * expert_gate_up.shape[0]
    capacity = max(2, (tok_count * top_count * 9 + 8 * experts_all - 1) // (8 * experts_all))
    hidden_width = expert_down.shape[1]

    pack = jnp.concatenate([expert_ids.T.astype(F32), route_weights.T], axis=0)
    meta = lax.all_gather(pack, ("row", "col"), axis=0, tiled=False)
    tokens_col = lax.all_gather(tokens, "col", axis=0, tiled=True)
    pass_slice = lax.all_gather(document_vectors, "row", axis=1, tiled=True)
    query_full = lax.all_gather(question_vectors, "col", axis=1, tiled=True)
    pass_full = lax.all_gather(pass_slice, "col", axis=0, tiled=True)

    ids = meta[:, :top_count].astype(jnp.int32)
    weights = meta[:, top_count:]

    block = col_size * capacity
    ids_row = lax.dynamic_slice_in_dim(ids, row * col_size, col_size, 0)
    plane = jnp.arange(row_size, dtype=jnp.int32) * col_size + col
    hit = jnp.any(ids_row[None] == plane[:, None, None, None], axis=2)
    slots = slot_counts(hit.reshape(-1, tok_count)).reshape(hit.shape)
    first = jnp.arange(col_size, dtype=jnp.int32)[None, :, None] * capacity
    place = jnp.where(hit, first + slots, -1).reshape(row_size, 1, col_size * tok_count)
    dispatch = (place == jnp.arange(block, dtype=jnp.int32)[None, :, None]).astype(BF)
    dispatch = dispatch.reshape(row_size * block, col_size * tok_count)
    outgoing = contract(dispatch, tokens_col, 1, 0).astype(BF)
    slot_inputs = lax.all_to_all(
        outgoing.reshape(row_size, block, model_width), "row", split_axis=0, concat_axis=0, tiled=True
    ).reshape(-1, model_width)

    scores = contract(query_full, pass_full, 1, 1) / sharpness_divisor
    peak = jnp.max(scores, axis=1, keepdims=True)
    grown = jnp.exp(scores - peak)
    total = jnp.sum(grown, axis=1, keepdims=True)
    onehot = (
        positive[:, None] == jnp.arange(pass_full.shape[0], dtype=jnp.int32)[None, :]
    ).astype(F32)
    dscore = ((grown / total - onehot) / sharpness_divisor).astype(BF)
    query_grad = contract(dscore, pass_full, 1, 0)
    cot_row = (query_grad / SEQ_LEN).astype(BF)
    cot = lax.all_gather(cot_row, "row", axis=0, tiled=True)

    mine = ids == me
    chosen = jnp.any(mine, axis=1)
    weight = jnp.sum(jnp.where(mine, weights, 0.0), axis=1)
    rank = slot_counts(chosen)
    where_to = jnp.where(
        chosen, jnp.arange(devices_all, dtype=jnp.int32)[:, None] * capacity + rank, -1
    )
    where_to = where_to.reshape(-1, SEQ_LEN).T
    weight = weight.reshape(-1, SEQ_LEN).T
    slot_ids = jnp.arange(devices_all * capacity, dtype=jnp.int32)[:, None]
    spread = jnp.zeros((devices_all * capacity, where_to.shape[1]), F32)
    for i in range(SEQ_LEN):
        spread = spread + jnp.where(slot_ids == where_to[i][None, :], weight[i][None, :], 0.0)
    spread = spread.astype(BF)

    gate_up = expert_gate_up[0]
    down = expert_down[0]
    projected = contract(slot_inputs, gate_up, 1, 0)
    gate_part = projected[:, :hidden_width]
    up_part = projected[:, hidden_width:]
    sigmoid_gate = jax.nn.sigmoid(gate_part)
    activated = gate_part * sigmoid_gate
    hidden = (activated * up_part).astype(BF)
    cot_down = contract(cot, down, 1, 1).astype(BF)
    hidden_grad = contract(spread, cot_down, 1, 0)
    slope = sigmoid_gate * (1.0 + gate_part * (1.0 - sigmoid_gate))
    pre_grad = jnp.concatenate(
        [hidden_grad * up_part * slope, hidden_grad * activated], axis=1
    ).astype(BF)
    input_grad = contract(pre_grad, gate_up, 1, 1).astype(BF)
    returned = lax.all_to_all(
        input_grad.reshape(row_size, block, model_width), "row", split_axis=0, concat_axis=0, tiled=True
    ).reshape(-1, model_width)
    gate_up_grad = contract(slot_inputs, pre_grad, 0, 0).astype(BF)
    hidden_by_query = contract(hidden, spread, 0, 0).astype(BF)
    down_grad = contract(hidden_by_query, cot, 1, 0).astype(BF)

    partial = contract(dispatch, returned, 0, 0).astype(BF)
    summed = lax.psum_scatter(partial, "col", scatter_dimension=0, tiled=True)
    per_dev = tok_count // SEQ_LEN
    cot_own = lax.dynamic_slice_in_dim(cot_row, col * per_dev, per_dev, 0)
    cot_tok = jnp.repeat(cot_own, SEQ_LEN, axis=0)
    token_grad = (cot_tok.astype(F32) + summed.astype(F32)).astype(BF)

    pass_count = document_vectors.shape[0]
    dscore_col = lax.dynamic_slice_in_dim(dscore, col * pass_count, pass_count, 1)
    passage_term = contract(dscore_col, query_full, 0, 0)
    passage_grad = lax.psum_scatter(
        passage_term.astype(BF), "row", scatter_dimension=1, tiled=True
    ).astype(F32)
    return (passage_grad, token_grad, gate_up_grad[None], down_grad[None])


def solution(mesh):
    in_specs = (
        P("row", "col"),
        P("col", "row"),
        P("row"),
        P(("row", "col"), None),
        P(("row", "col"), None),
        P(("row", "col"), None),
        P(("row", "col"), None, None),
        P(("row", "col"), None, None),
    )
    out_specs = (
        P("col", "row"),
        P(("row", "col"), None),
        P(("row", "col"), None, None),
        P(("row", "col"), None, None),
    )
    return jax.shard_map(shards, mesh=mesh, in_specs=in_specs, out_specs=out_specs, check_vma=False)
```

```python
import functools

import jax
import jax.numpy as jnp
from jax import lax
from jax.experimental import pallas as pl
from jax.experimental.pallas import tpu as pltpu
from jax.sharding import PartitionSpec as P

SEQ_LEN = 8


sharpness_divisor = 0.02

BF = jnp.bfloat16
F32 = jnp.float32


def contract(a, b, da, db):
    return lax.dot_general(a, b, (((da,), (db,)), ((), ())), preferred_element_type=F32)


def slot_counts(hit):
    tok = hit.shape[1]
    earlier = (
        lax.broadcasted_iota(jnp.int32, (tok, tok), 0)
        < lax.broadcasted_iota(jnp.int32, (tok, tok), 1)
    ).astype(BF)
    return contract(hit.astype(BF), earlier, 1, 0).astype(jnp.int32)


MESH = pl.DeviceIdType.MESH
PIECES = 2
CHUNKS = 2


def greet(rows, cols):
    row, col = lax.axis_index("row"), lax.axis_index("col")
    barrier = pltpu.get_barrier_semaphore()
    for s in range(1, rows):
        pl.semaphore_signal(
            barrier, inc=1, device_id=(lax.rem(row + s, rows), col), device_id_type=MESH
        )
    for s in range(1, cols):
        pl.semaphore_signal(
            barrier, inc=1, device_id=(row, lax.rem(col + s, cols)), device_id_type=MESH
        )
    pl.semaphore_wait(barrier, rows + cols - 2)


def gather_kernel(
    rows, cols, tok_ref, doc_ref, qry_ref, pack_ref, tok_out, doc_out, qry_out, pack_out,
    own_sem, tok_send, tok_recv, zs_send, zs_recv, rs_send, rs_recv,
):
    row, col = lax.axis_index("row"), lax.axis_index("col")
    n_tok = tok_ref.shape[0]
    n_doc, w_doc = doc_ref.shape
    w_qry = qry_ref.shape[1]
    piece = n_tok // PIECES

    def doc_at(r, c):
        return doc_out.at[
            pl.ds(pl.multiple_of(c * n_doc, n_doc), n_doc),
            pl.ds(pl.multiple_of(r * w_doc, w_doc), w_doc),
        ]

    def doc_strip(r):
        return doc_out.at[:, pl.ds(pl.multiple_of(r * w_doc, w_doc), w_doc)]

    def qry_at(c):
        return qry_out.at[:, pl.ds(pl.multiple_of(c * w_qry, w_qry), w_qry)]

    def pack_strip(r):
        return pack_out.at[pl.ds(r * cols, cols)]

    def tok_at(c, f):
        return tok_out.at[pl.ds(pl.multiple_of(c * n_tok + f * piece, piece), piece)]

    own = [
        pltpu.make_async_copy(pack_ref, pack_out.at[row * cols + col], own_sem.at[0]),
        pltpu.make_async_copy(doc_ref, doc_at(row, col), own_sem.at[1]),
        pltpu.make_async_copy(qry_ref, qry_at(col), own_sem.at[2]),
        pltpu.make_async_copy(
            tok_ref, tok_out.at[pl.ds(pl.multiple_of(col * n_tok, n_tok), n_tok)], own_sem.at[3]
        ),
    ]
    for copy in own:
        copy.start()
    greet(rows, cols)

    def along_col(kind, src, dst, s, origin, to):
        return pltpu.make_async_remote_copy(
            src_ref=src, dst_ref=dst, send_sem=zs_send.at[kind, s], recv_sem=zs_recv.at[kind, origin],
            device_id=(row, to), device_id_type=MESH,
        )

    def small(kind, s, origin, to):
        if kind == 0:
            return along_col(0, pack_ref, pack_out.at[row * cols + origin], s, origin, to)
        if kind == 1:
            return along_col(1, doc_ref, doc_at(row, origin), s, origin, to)
        return along_col(2, qry_ref, qry_at(origin), s, origin, to)

    for kind in range(3):
        for s in range(1, cols):
            small(kind, s, col, lax.rem(col + s, cols)).start()

    def hop(step, way, f, block, src, to):
        return pltpu.make_async_remote_copy(
            src_ref=src, dst_ref=tok_at(block, f), send_sem=tok_send.at[way, step, f],
            recv_sem=tok_recv.at[block, f], device_id=(row, to), device_id_type=MESH,
        )

    ways = ((0, 1), (1, -1))

    def can_send(way):
        return col < cols - 1 if way == 0 else col > 0

    for f in range(PIECES):
        for way, d in ways:
            @pl.when(can_send(way))
            def _():
                hop(0, way, f, col, tok_ref.at[pl.ds(f * piece, piece)], col + d).start()

    def on(kind, s, origin, to):
        strip = pack_strip(origin) if kind == 0 else doc_strip(origin)
        return pltpu.make_async_remote_copy(
            src_ref=strip, dst_ref=strip, send_sem=rs_send.at[kind, s],
            recv_sem=rs_recv.at[kind, origin], device_id=(to, col), device_id_type=MESH,
        )

    for kind in range(2):
        own[kind].wait()
        for s in range(1, cols):
            origin = lax.rem(col + s, cols)
            small(kind, s, origin, origin).wait_recv()
        for s in range(1, rows):
            on(kind, s, row, lax.rem(row + s, rows)).start()

    for step in range(1, cols):
        for f in range(PIECES):
            for way, d in ways:
                block = col - d * step
                came = block >= 0 if way == 0 else block < cols

                @pl.when(came)
                def _():
                    hop(step, way, f, block, tok_at(block, f), block).wait_recv()

                @pl.when(jnp.logical_and(came, can_send(way)))
                def _():
                    hop(step, way, f, block, tok_at(block, f), col + d).start()

    for step in range(cols):
        for f in range(PIECES):
            for way, d in ways:
                block = col - d * step
                came = block >= 0 if way == 0 else block < cols

                @pl.when(jnp.logical_and(came, can_send(way)))
                def _():
                    hop(step, way, f, block, tok_at(block, f), col + d).wait_send()

    for s in range(1, cols):
        origin = lax.rem(col + s, cols)
        small(2, s, origin, origin).wait_recv()
    for kind in range(3):
        for s in range(1, cols):
            small(kind, s, col, lax.rem(col + s, cols)).wait_send()
    for kind in range(2):
        for s in range(1, rows):
            origin = lax.rem(row + s, rows)
            on(kind, s, origin, origin).wait_recv()
        for s in range(1, rows):
            on(kind, s, row, lax.rem(row + s, rows)).wait_send()
    own[2].wait()
    own[3].wait()


def gather_all(rows, cols, tokens, documents, questions, pack):
    n_tok, width = tokens.shape
    n_doc, w_doc = documents.shape
    n_qry, w_qry = questions.shape
    dma = pltpu.SemaphoreType.DMA
    vmem = pl.BlockSpec(memory_space=pltpu.VMEM)
    return pl.pallas_call(
        functools.partial(gather_kernel, rows, cols),
        out_shape=(
            jax.ShapeDtypeStruct((cols * n_tok, width), tokens.dtype),
            jax.ShapeDtypeStruct((cols * n_doc, rows * w_doc), documents.dtype),
            jax.ShapeDtypeStruct((n_qry, cols * w_qry), questions.dtype),
            jax.ShapeDtypeStruct((rows * cols,) + pack.shape, pack.dtype),
        ),
        in_specs=[vmem] * 4,
        out_specs=[pl.BlockSpec(memory_space=pl.ANY)] * 4,
        scratch_shapes=[
            dma((4,)),
            dma((2, cols, PIECES)),
            dma((cols, PIECES)),
            dma((3, cols)),
            dma((3, cols)),
            dma((2, rows)),
            dma((2, rows)),
        ],
        compiler_params=pltpu.CompilerParams(collective_id=0, has_side_effects=True),
        name="gather_all",
    )(tokens, documents, questions, pack)


def shards(
    question_vectors,
    document_vectors,
    positive,
    tokens,
    expert_ids,
    route_weights,
    expert_gate_up,
    expert_down,
):
    row_size = lax.axis_size("row")
    col_size = lax.axis_size("col")
    row = lax.axis_index("row")
    col = lax.axis_index("col")
    devices_all = row_size * col_size
    me = row * col_size + col
    tok_count, model_width = tokens.shape
    top_count = expert_ids.shape[1]
    experts_all = devices_all * expert_gate_up.shape[0]
    capacity = max(2, (tok_count * top_count * 9 + 8 * experts_all - 1) // (8 * experts_all))
    hidden_width = expert_down.shape[1]

    pack = jnp.concatenate([expert_ids.T.astype(F32), route_weights.T], axis=0)
    tokens_col, pass_full, query_full, meta = gather_all(
        row_size, col_size, tokens, document_vectors, question_vectors, pack
    )

    ids = meta[:, :top_count].astype(jnp.int32)
    weights = meta[:, top_count:]

    block = col_size * capacity
    ids_row = lax.dynamic_slice_in_dim(ids, row * col_size, col_size, 0)
    plane = jnp.arange(row_size, dtype=jnp.int32) * col_size + col
    hit = jnp.any(ids_row[None] == plane[:, None, None, None], axis=2)
    slots = slot_counts(hit.reshape(-1, tok_count)).reshape(hit.shape)
    first = jnp.arange(col_size, dtype=jnp.int32)[None, :, None] * capacity
    place = jnp.where(hit, first + slots, -1).reshape(row_size, 1, col_size * tok_count)
    dispatch = (place == jnp.arange(block, dtype=jnp.int32)[None, :, None]).astype(BF)
    dispatch = dispatch.reshape(row_size * block, col_size * tok_count)
    outgoing = contract(dispatch, tokens_col, 1, 0).astype(BF)
    slot_inputs = lax.all_to_all(
        outgoing.reshape(row_size, block, model_width), "row", split_axis=0, concat_axis=0, tiled=True
    ).reshape(-1, model_width)

    scores = contract(query_full, pass_full, 1, 1) / sharpness_divisor
    peak = jnp.max(scores, axis=1, keepdims=True)
    grown = jnp.exp(scores - peak)
    total = jnp.sum(grown, axis=1, keepdims=True)
    onehot = (
        positive[:, None] == jnp.arange(pass_full.shape[0], dtype=jnp.int32)[None, :]
    ).astype(F32)
    dscore = ((grown / total - onehot) / sharpness_divisor).astype(BF)
    query_grad = contract(dscore, pass_full, 1, 0)
    cot_row = (query_grad / SEQ_LEN).astype(BF)
    cot = lax.all_gather(cot_row, "row", axis=0, tiled=True)

    mine = ids == me
    chosen = jnp.any(mine, axis=1)
    weight = jnp.sum(jnp.where(mine, weights, 0.0), axis=1)
    rank = slot_counts(chosen)
    where_to = jnp.where(
        chosen, jnp.arange(devices_all, dtype=jnp.int32)[:, None] * capacity + rank, -1
    )
    where_to = where_to.reshape(-1, SEQ_LEN).T
    weight = weight.reshape(-1, SEQ_LEN).T
    slot_ids = jnp.arange(devices_all * capacity, dtype=jnp.int32)[:, None]
    spread = jnp.zeros((devices_all * capacity, where_to.shape[1]), F32)
    for i in range(SEQ_LEN):
        spread = spread + jnp.where(slot_ids == where_to[i][None, :], weight[i][None, :], 0.0)
    spread = spread.astype(BF)

    gate_up = expert_gate_up[0]
    down = expert_down[0]
    projected = contract(slot_inputs, gate_up, 1, 0)
    gate_part = projected[:, :hidden_width]
    up_part = projected[:, hidden_width:]
    sigmoid_gate = jax.nn.sigmoid(gate_part)
    activated = gate_part * sigmoid_gate
    hidden = (activated * up_part).astype(BF)
    cot_down = contract(cot, down, 1, 1).astype(BF)
    hidden_grad = contract(spread, cot_down, 1, 0)
    slope = sigmoid_gate * (1.0 + gate_part * (1.0 - sigmoid_gate))
    pre_grad = jnp.concatenate(
        [hidden_grad * up_part * slope, hidden_grad * activated], axis=1
    ).astype(BF)
    chunks = []
    step = model_width // CHUNKS
    for k in range(CHUNKS):
        input_grad = contract(pre_grad, gate_up[k * step : (k + 1) * step], 1, 1).astype(BF)
        chunks.append(
            lax.all_to_all(
                input_grad.reshape(row_size, block, step), "row", split_axis=0, concat_axis=0, tiled=True
            ).reshape(-1, step)
        )
    gate_up_grad = contract(slot_inputs, pre_grad, 0, 0).astype(BF)
    hidden_by_query = contract(hidden, spread, 0, 0).astype(BF)
    down_grad = contract(hidden_by_query, cot, 1, 0).astype(BF)

    summed = jnp.concatenate(
        [
            lax.psum_scatter(
                contract(dispatch, returned, 0, 0).astype(BF), "col", scatter_dimension=0, tiled=True
            )
            for returned in chunks
        ],
        axis=1,
    )
    per_dev = tok_count // SEQ_LEN
    cot_own = lax.dynamic_slice_in_dim(cot_row, col * per_dev, per_dev, 0)
    cot_tok = jnp.repeat(cot_own, SEQ_LEN, axis=0)
    token_grad = (cot_tok.astype(F32) + summed.astype(F32)).astype(BF)

    pass_count = document_vectors.shape[0]
    dscore_col = lax.dynamic_slice_in_dim(dscore, col * pass_count, pass_count, 1)
    passage_term = contract(dscore_col, query_full, 0, 0)
    passage_grad = lax.psum_scatter(
        passage_term.astype(BF), "row", scatter_dimension=1, tiled=True
    ).astype(F32)
    return (passage_grad, token_grad, gate_up_grad[None], down_grad[None])


def solution(mesh):
    in_specs = (
        P("row", "col"),
        P("col", "row"),
        P("row"),
        P(("row", "col"), None),
        P(("row", "col"), None),
        P(("row", "col"), None),
        P(("row", "col"), None, None),
        P(("row", "col"), None, None),
    )
    out_specs = (
        P("col", "row"),
        P(("row", "col"), None),
        P(("row", "col"), None, None),
        P(("row", "col"), None, None),
    )
    return jax.shard_map(shards, mesh=mesh, in_specs=in_specs, out_specs=out_specs, check_vma=False)
```

```python
import functools

import jax
import jax.numpy as jnp
from jax import lax
from jax.experimental import pallas as pl
from jax.experimental.pallas import tpu as pltpu
from jax.sharding import PartitionSpec as P

SEQ_LEN = 8


sharpness_divisor = 0.02


BF = jnp.bfloat16
F32 = jnp.float32


def contract(a, b, da, db):
    return lax.dot_general(a, b, (((da,), (db,)), ((), ())), preferred_element_type=F32)


def slot_counts(hit):
    tok = hit.shape[1]
    earlier = (
        lax.broadcasted_iota(jnp.int32, (tok, tok), 0)
        < lax.broadcasted_iota(jnp.int32, (tok, tok), 1)
    ).astype(BF)
    return contract(hit.astype(BF), earlier, 1, 0).astype(jnp.int32)


MESH = pl.DeviceIdType.MESH
PIECES = 2
CHUNKS = 2


def greet(rows, cols):
    row, col = lax.axis_index("row"), lax.axis_index("col")
    barrier = pltpu.get_barrier_semaphore()
    for s in range(1, rows):
        pl.semaphore_signal(
            barrier, inc=1, device_id=(lax.rem(row + s, rows), col), device_id_type=MESH
        )
    for s in range(1, cols):
        pl.semaphore_signal(
            barrier, inc=1, device_id=(row, lax.rem(col + s, cols)), device_id_type=MESH
        )
    pl.semaphore_wait(barrier, rows + cols - 2)


def gather_kernel(
    rows, cols, tok_ref, doc_ref, qry_ref, pack_ref, tok_out, doc_out, qry_out, pack_out,
    own_sem, tok_send, tok_recv, zs_send, zs_recv, rs_send, rs_recv,
):
    row, col = lax.axis_index("row"), lax.axis_index("col")
    n_tok = tok_ref.shape[0]
    n_doc, w_doc = doc_ref.shape
    w_qry = qry_ref.shape[1]
    piece = n_tok // PIECES

    def doc_at(r, c):
        return doc_out.at[
            pl.ds(pl.multiple_of(c * n_doc, n_doc), n_doc),
            pl.ds(pl.multiple_of(r * w_doc, w_doc), w_doc),
        ]

    def doc_strip(r):
        return doc_out.at[:, pl.ds(pl.multiple_of(r * w_doc, w_doc), w_doc)]

    def qry_at(c):
        return qry_out.at[:, pl.ds(pl.multiple_of(c * w_qry, w_qry), w_qry)]

    def pack_strip(r):
        return pack_out.at[pl.ds(r * cols, cols)]

    def tok_at(c, f):
        return tok_out.at[pl.ds(pl.multiple_of(c * n_tok + f * piece, piece), piece)]

    own = [
        pltpu.make_async_copy(pack_ref, pack_out.at[row * cols + col], own_sem.at[0]),
        pltpu.make_async_copy(doc_ref, doc_at(row, col), own_sem.at[1]),
        pltpu.make_async_copy(qry_ref, qry_at(col), own_sem.at[2]),
        pltpu.make_async_copy(
            tok_ref, tok_out.at[pl.ds(pl.multiple_of(col * n_tok, n_tok), n_tok)], own_sem.at[3]
        ),
    ]
    for copy in own:
        copy.start()
    greet(rows, cols)

    def along_col(kind, src, dst, s, origin, to):
        return pltpu.make_async_remote_copy(
            src_ref=src, dst_ref=dst, send_sem=zs_send.at[kind, s], recv_sem=zs_recv.at[kind, origin],
            device_id=(row, to), device_id_type=MESH,
        )

    def small(kind, s, origin, to):
        if kind == 0:
            return along_col(0, pack_ref, pack_out.at[row * cols + origin], s, origin, to)
        if kind == 1:
            return along_col(1, doc_ref, doc_at(row, origin), s, origin, to)
        return along_col(2, qry_ref, qry_at(origin), s, origin, to)

    for kind in range(3):
        for s in range(1, cols):
            small(kind, s, col, lax.rem(col + s, cols)).start()

    def hop(step, way, f, block, src, to):
        return pltpu.make_async_remote_copy(
            src_ref=src, dst_ref=tok_at(block, f), send_sem=tok_send.at[way, step, f],
            recv_sem=tok_recv.at[block, f], device_id=(row, to), device_id_type=MESH,
        )

    ways = ((0, 1), (1, -1))

    def can_send(way):
        return col < cols - 1 if way == 0 else col > 0

    for f in range(PIECES):
        for way, d in ways:
            @pl.when(can_send(way))
            def _():
                hop(0, way, f, col, tok_ref.at[pl.ds(f * piece, piece)], col + d).start()

    def on(kind, s, origin, to):
        strip = pack_strip(origin) if kind == 0 else doc_strip(origin)
        return pltpu.make_async_remote_copy(
            src_ref=strip, dst_ref=strip, send_sem=rs_send.at[kind, s],
            recv_sem=rs_recv.at[kind, origin], device_id=(to, col), device_id_type=MESH,
        )

    for kind in range(2):
        own[kind].wait()
        for s in range(1, cols):
            origin = lax.rem(col + s, cols)
            small(kind, s, origin, origin).wait_recv()
        for s in range(1, rows):
            on(kind, s, row, lax.rem(row + s, rows)).start()

    for step in range(1, cols):
        for f in range(PIECES):
            for way, d in ways:
                block = col - d * step
                came = block >= 0 if way == 0 else block < cols

                @pl.when(came)
                def _():
                    hop(step, way, f, block, tok_at(block, f), block).wait_recv()

                @pl.when(jnp.logical_and(came, can_send(way)))
                def _():
                    hop(step, way, f, block, tok_at(block, f), col + d).start()

    for step in range(cols):
        for f in range(PIECES):
            for way, d in ways:
                block = col - d * step
                came = block >= 0 if way == 0 else block < cols

                @pl.when(jnp.logical_and(came, can_send(way)))
                def _():
                    hop(step, way, f, block, tok_at(block, f), col + d).wait_send()

    for s in range(1, cols):
        origin = lax.rem(col + s, cols)
        small(2, s, origin, origin).wait_recv()
    for kind in range(3):
        for s in range(1, cols):
            small(kind, s, col, lax.rem(col + s, cols)).wait_send()
    for kind in range(2):
        for s in range(1, rows):
            origin = lax.rem(row + s, rows)
            on(kind, s, origin, origin).wait_recv()
        for s in range(1, rows):
            on(kind, s, row, lax.rem(row + s, rows)).wait_send()
    own[2].wait()
    own[3].wait()


def passed(value, axis, n, s):
    return lax.ppermute(value, axis, [(i, (i + s) % n) for i in range(n)])


def shared_sums(value, axis, n, dim):
    here = lax.axis_index(axis)
    width = value.shape[dim] // n
    total = lax.dynamic_slice_in_dim(value, here * width, width, dim).astype(F32)
    for s in range(1, n):
        share = lax.dynamic_slice_in_dim(value, lax.rem(here + s, n) * width, width, dim)
        total = total + passed(share, axis, n, s).astype(F32)
    return total


def gather_all(rows, cols, tokens, documents, questions, pack):
    n_tok, width = tokens.shape
    n_doc, w_doc = documents.shape
    n_qry, w_qry = questions.shape
    dma = pltpu.SemaphoreType.DMA
    vmem = pl.BlockSpec(memory_space=pltpu.VMEM)
    return pl.pallas_call(
        functools.partial(gather_kernel, rows, cols),
        out_shape=(
            jax.ShapeDtypeStruct((cols * n_tok, width), tokens.dtype),
            jax.ShapeDtypeStruct((cols * n_doc, rows * w_doc), documents.dtype),
            jax.ShapeDtypeStruct((n_qry, cols * w_qry), questions.dtype),
            jax.ShapeDtypeStruct((rows * cols,) + pack.shape, pack.dtype),
        ),
        in_specs=[vmem] * 4,
        out_specs=[pl.BlockSpec(memory_space=pl.ANY)] * 4,
        scratch_shapes=[
            dma((4,)),
            dma((2, cols, PIECES)),
            dma((cols, PIECES)),
            dma((3, cols)),
            dma((3, cols)),
            dma((2, rows)),
            dma((2, rows)),
        ],
        compiler_params=pltpu.CompilerParams(collective_id=0, has_side_effects=True),
        name="gather_all",
    )(tokens, documents, questions, pack)


def shards(
    question_vectors,
    document_vectors,
    positive,
    tokens,
    expert_ids,
    route_weights,
    expert_gate_up,
    expert_down,
):
    row_size = lax.axis_size("row")
    col_size = lax.axis_size("col")
    row = lax.axis_index("row")
    col = lax.axis_index("col")
    devices_all = row_size * col_size
    me = row * col_size + col
    tok_count, model_width = tokens.shape
    top_count = expert_ids.shape[1]
    experts_all = devices_all * expert_gate_up.shape[0]
    capacity = max(2, (tok_count * top_count * 9 + 8 * experts_all - 1) // (8 * experts_all))
    hidden_width = expert_down.shape[1]

    pack = jnp.concatenate([expert_ids.T.astype(F32), route_weights.T], axis=0)
    tokens_col, pass_full, query_full, meta = gather_all(
        row_size, col_size, tokens, document_vectors, question_vectors, pack
    )

    ids = meta[:, :top_count].astype(jnp.int32)
    weights = meta[:, top_count:]

    block = col_size * capacity
    ids_row = lax.dynamic_slice_in_dim(ids, row * col_size, col_size, 0)
    plane = jnp.arange(row_size, dtype=jnp.int32) * col_size + col
    hit = jnp.any(ids_row[None] == plane[:, None, None, None], axis=2)
    slots = slot_counts(hit.reshape(-1, tok_count)).reshape(hit.shape)
    first = jnp.arange(col_size, dtype=jnp.int32)[None, :, None] * capacity
    place = jnp.where(hit, first + slots, -1).reshape(row_size, 1, col_size * tok_count)
    dispatch = (place == jnp.arange(block, dtype=jnp.int32)[None, :, None]).astype(BF)
    dispatch = dispatch.reshape(row_size * block, col_size * tok_count)
    outgoing = contract(dispatch, tokens_col, 1, 0).astype(BF)
    slot_inputs = lax.all_to_all(
        outgoing.reshape(row_size, block, model_width), "row", split_axis=0, concat_axis=0, tiled=True
    ).reshape(-1, model_width)

    scores = contract(query_full, pass_full, 1, 1) / sharpness_divisor
    peak = jnp.max(scores, axis=1, keepdims=True)
    grown = jnp.exp(scores - peak)
    total = jnp.sum(grown, axis=1, keepdims=True)
    onehot = (
        positive[:, None] == jnp.arange(pass_full.shape[0], dtype=jnp.int32)[None, :]
    ).astype(F32)
    dscore = ((grown / total - onehot) / sharpness_divisor).astype(BF)
    query_grad = contract(dscore, pass_full, 1, 0)
    cot_row = (query_grad / SEQ_LEN).astype(BF)
    cot = jnp.concatenate(
        [cot_row] + [passed(cot_row, "row", row_size, s) for s in range(1, row_size)], axis=0
    )

    mine = ids == me
    chosen = jnp.any(mine, axis=1)
    weight = jnp.sum(jnp.where(mine, weights, 0.0), axis=1)
    rank = slot_counts(chosen)
    where_to = jnp.where(
        chosen, jnp.arange(devices_all, dtype=jnp.int32)[:, None] * capacity + rank, -1
    )
    order = lax.rem(row + row_size - jnp.arange(row_size, dtype=jnp.int32), row_size)
    where_to = where_to.reshape(row_size, -1)[order].reshape(-1, SEQ_LEN).T
    weight = weight.reshape(row_size, -1)[order].reshape(-1, SEQ_LEN).T
    slot_ids = jnp.arange(devices_all * capacity, dtype=jnp.int32)[:, None]
    spread = jnp.zeros((devices_all * capacity, where_to.shape[1]), F32)
    for i in range(SEQ_LEN):
        spread = spread + jnp.where(slot_ids == where_to[i][None, :], weight[i][None, :], 0.0)
    spread = spread.astype(BF)

    gate_up = expert_gate_up[0]
    down = expert_down[0]
    projected = contract(slot_inputs, gate_up, 1, 0)
    gate_part = projected[:, :hidden_width]
    up_part = projected[:, hidden_width:]
    sigmoid_gate = jax.nn.sigmoid(gate_part)
    activated = gate_part * sigmoid_gate
    hidden = (activated * up_part).astype(BF)
    cot_down = contract(cot, down, 1, 1).astype(BF)
    hidden_grad = contract(spread, cot_down, 1, 0)
    slope = sigmoid_gate * (1.0 + gate_part * (1.0 - sigmoid_gate))
    pre_grad = jnp.concatenate(
        [hidden_grad * up_part * slope, hidden_grad * activated], axis=1
    ).astype(BF)
    chunks = []
    step = model_width // CHUNKS
    for k in range(CHUNKS):
        input_grad = contract(pre_grad, gate_up[k * step : (k + 1) * step], 1, 1).astype(BF)
        chunks.append(
            lax.all_to_all(
                input_grad.reshape(row_size, block, step), "row", split_axis=0, concat_axis=0, tiled=True
            ).reshape(-1, step)
        )
    gate_up_grad = contract(slot_inputs, pre_grad, 0, 0).astype(BF)
    hidden_by_query = contract(hidden, spread, 0, 0).astype(BF)
    down_grad = contract(hidden_by_query, cot, 1, 0).astype(BF)

    summed = jnp.concatenate(
        [
            shared_sums(contract(dispatch, returned, 0, 0).astype(BF), "col", col_size, 0)
            for returned in chunks
        ],
        axis=1,
    )
    per_dev = tok_count // SEQ_LEN
    cot_own = lax.dynamic_slice_in_dim(cot_row, col * per_dev, per_dev, 0)
    cot_tok = jnp.repeat(cot_own, SEQ_LEN, axis=0)
    token_grad = (cot_tok.astype(F32) + summed).astype(BF)

    pass_count = document_vectors.shape[0]
    dscore_col = lax.dynamic_slice_in_dim(dscore, col * pass_count, pass_count, 1)
    passage_term = contract(dscore_col, query_full, 0, 0)
    passage_grad = shared_sums(passage_term.astype(BF), "row", row_size, 1)
    return (passage_grad, token_grad, gate_up_grad[None], down_grad[None])


def solution(mesh):
    in_specs = (
        P("row", "col"),
        P("col", "row"),
        P("row"),
        P(("row", "col"), None),
        P(("row", "col"), None),
        P(("row", "col"), None),
        P(("row", "col"), None, None),
        P(("row", "col"), None, None),
    )
    out_specs = (
        P("col", "row"),
        P(("row", "col"), None),
        P(("row", "col"), None, None),
        P(("row", "col"), None, None),
    )
    return jax.shard_map(shards, mesh=mesh, in_specs=in_specs, out_specs=out_specs, check_vma=False)
```
